32 devices in a mesh: clip: 2 (over x), seq: 4 (over y, core), sub: 4 (over z).
Axes of the slice: x: 2, y: 2, z: 4, core: 2. Of those that a mesh axis runs over, the one named last changes fastest.
Arguments:
- latent: bfloat16 [4096, 1536], P(('clip', 'seq', 'sub')), parts along dimension 0, may hold values from -6 to 6
- cond_kv: bfloat16 [1024, 2, 1024], P(('clip', 'seq', 'sub')), parts along dimension 0, may hold values from -6 to 6
- qkv_weight: bfloat16 [1536, 3072], replicated, may hold values from -0.15625 to 0.15625
- qk_gain: float32 [2, 16, 64], replicated, may hold values from 0.5 to 16
- out_weight: bfloat16 [1024, 1536], replicated, may hold values from -0.1875 to 0.1875
Outputs:
- output: bfloat16 [4096, 1536], P(('clip', 'seq', 'sub')), parts along dimension 0
The draws below stay inside these ranges and needn't reach their ends.
There are 2 independent parts, one for each index of `clip`. The reference program is written for one: setup_inputs(seed, part) draws one part's arguments, and reference() takes and returns one part's arrays. A program takes and returns all parts, laid end to end along the dimension named above; an argument that names none is the same for every part. Nothing has to cross between parts.
All inputs are finite; a program needn't handle non-finite values.
Results may differ from the reference program's by a relative error of at most 0.008.
The reference program's roundings to bfloat16 on the way count: a program that leaves them out, or rounds other values in their place, can miss the bound.
Values may be sent and summed in bfloat16 or wider, within the bound.
A program may use at most 320 MiB of HBM per device.

```python
import math
import jax
import jax.numpy as jnp
from jax import lax

D = 1536
HEADS = 16
HDIM = 64
HD = 1024
SEQLEN = 2048
CTX = 512


def draw_qk_gain(key, part):
    first = jax.random.fold_in(key, 0)
    base = jnp.exp(jax.random.uniform(first, (2, HEADS, HDIM), jnp.float32, math.log(0.7), math.log(2.5)))
    return base.astype(jnp.float32)


def block_levels(key, shape, shards, low, largest):
    def one(position, blocks):
        steps = jax.random.uniform(jax.random.fold_in(jax.random.fold_in(key, 6), position), (blocks,), jnp.float32, low / len(shards), largest / len(shards))
        return jnp.repeat(jnp.exp(steps), shape[position] // blocks).reshape((-1,) + (1,) * (len(shape) - position - 1))

    loudness = one(*shards[0])
    for cut in shards[1:]:
        loudness = loudness * one(*cut)
    return loudness


def scatter_about(rng, shape, spread, most, cuts=(), kind=jnp.bfloat16):
    drawn = spread * jax.random.normal(rng, shape, jnp.float32)
    if cuts:
        drawn = drawn * block_levels(rng, shape, cuts, -0.22, 0.18)
    return jnp.clip(drawn, -most, most).astype(kind)


def setup_inputs(seed: int = 0, part: int = 0) -> dict:
    arg_keys = jax.random.split(jax.random.key(seed), 6)
    part_splits = jax.random.split(jax.random.fold_in(arg_keys[5], part), 6)
    return {
        "latent": scatter_about(part_splits[0], (SEQLEN, D), 1.0, 6.0, ((0, 16),)),
        "cond_kv": scatter_about(part_splits[1], (CTX, 2, HD), 1.0, 6.0, ((0, 16),)),
        "qkv_weight": scatter_about(arg_keys[2], (D, 3 * HD), D ** -0.5, 0.15625),
        "qk_gain": draw_qk_gain(jax.random.fold_in(arg_keys[5], 71), part),
        "out_weight": scatter_about(arg_keys[4], (HD, D), HD ** -0.5, 0.1875),
    }


def rms_gain(field, gain):
    return field * lax.rsqrt(lax.optimization_barrier(jnp.mean(field * field, axis=-1, keepdims=True)) + 1e-06) * gain

def reference(latent, cond_kv, qkv_weight, qk_gain, out_weight):
    proj = jnp.dot(latent, qkv_weight, preferred_element_type=jnp.float32).reshape(SEQLEN, 3, HEADS, HDIM)
    query = rms_gain(proj[:, 0], qk_gain[0]).astype(jnp.bfloat16)
    keyed = rms_gain(proj[:, 1], qk_gain[1]).astype(jnp.bfloat16)
    valued = proj[:, 2].astype(jnp.bfloat16)
    cond = cond_kv.reshape(CTX, 2, HEADS, HDIM)
    cond_key = rms_gain(cond[:, 0].astype(jnp.float32), qk_gain[1]).astype(jnp.bfloat16)
    keys_all = jnp.concatenate([keyed, cond_key], axis=0).transpose(1, 0, 2)
    values_all = jnp.concatenate([valued, cond[:, 1]], axis=0).transpose(1, 0, 2)
    query_heads = query.transpose(1, 0, 2)
    scale = 1.0 / math.sqrt(HDIM)
    qblock = math.gcd(SEQLEN, 2048)

    def one_head(operands):
        q_head, k_head, v_head = operands
        blocks = q_head.reshape(SEQLEN // qblock, qblock, HDIM)

        def one_block(q_block):
            scores = jnp.dot(q_block, k_head.T, preferred_element_type=jnp.float32) * scale
            highest = lax.optimization_barrier(jnp.max(scores, axis=-1, keepdims=True))
            expd = jnp.exp(scores - highest)
            total = lax.optimization_barrier(jnp.sum(expd, axis=-1, keepdims=True))
            weights = expd.astype(jnp.bfloat16)
            return jnp.dot(weights, v_head, preferred_element_type=jnp.float32) / total
        return lax.map(one_block, blocks).reshape(SEQLEN, HDIM)
    attended = lax.map(one_head, (query_heads, keys_all, values_all))
    attended = attended.transpose(1, 0, 2).reshape(SEQLEN, HEADS * HDIM).astype(jnp.bfloat16)
    return jnp.dot(attended, out_weight, preferred_element_type=jnp.float32).astype(jnp.bfloat16)
```

```python
import functools

import jax
import jax.numpy as jnp
from jax import lax
from jax.experimental import pallas as pl
from jax.experimental.pallas import tpu as pltpu
from jax.sharding import PartitionSpec as P


def rms_gain(field, gain):
    return field * lax.rsqrt(jnp.mean(field * field, axis=-1, keepdims=True) + 1e-06) * gain


def update(carry, query, key_block, value_block):
    highest, total, summed = carry
    scale = 1.0 / jnp.sqrt(jnp.float32(query.shape[-1]))
    scores = (
        jnp.einsum("qhd,khd->hqk", query, key_block, preferred_element_type=jnp.float32) * scale
    )
    new_high = jnp.maximum(highest, jnp.max(scores, axis=-1))
    expd = jnp.exp(scores - new_high[..., None])
    factor = jnp.exp(highest - new_high)
    total = total * factor + jnp.sum(expd, axis=-1)
    summed = summed * factor[..., None] + jnp.einsum(
        "hqk,khd->hqd", expd.astype(jnp.bfloat16), value_block, preferred_element_type=jnp.float32
    )
    return (new_high, total, summed)


def fold_rows(carry, query, keys_piece, values_piece, block_rows):
    count = keys_piece.shape[0] // block_rows
    key_blocks = keys_piece.reshape((count, block_rows) + keys_piece.shape[1:])
    value_blocks = values_piece.reshape((count, block_rows) + values_piece.shape[1:])

    def advance(state, pair):
        return (update(state, query, pair[0], pair[1]), None)

    carry, unused = lax.scan(advance, carry, (key_blocks, value_blocks))
    return carry


def arrange(sent, cond_sent, width):
    queries = sent.shape[0]
    local_heads = sent.shape[2] // width
    query = sent[:, 0].reshape(queries, local_heads, width)
    keyed = sent[:, 1].reshape(queries, local_heads, width)
    valued = sent[:, 2].reshape(queries, local_heads, width)
    cond_rows = cond_sent.shape[0]
    cond_key = cond_sent[:, 0].reshape(cond_rows, local_heads, width)
    cond_value = cond_sent[:, 1].reshape(cond_rows, local_heads, width)
    start_state = (
        jnp.full((local_heads, queries), -1e30, jnp.float32),
        jnp.zeros((local_heads, queries), jnp.float32),
        jnp.zeros((local_heads, queries, width), jnp.float32),
    )

    def absorb(carry, pieces, start):
        carry = fold_rows(carry, query, pieces[0], pieces[1], queries)
        return fold_rows(carry, query, pieces[2], pieces[3], cond_rows)

    return ((keyed, valued, cond_key, cond_value), start_state, absorb)


def finish(carry):
    highest, total, summed = carry
    attended = summed / total[..., None]
    local_heads, queries, width = attended.shape
    return attended.transpose(1, 0, 2).reshape(queries, local_heads * width).astype(jnp.bfloat16)


def local(latent, cond_kv, qkv_weight, qk_gain, out_weight):
    rows = latent.shape[0]
    heads = qk_gain.shape[1]
    width = qk_gain.shape[2]
    proj = jnp.dot(latent, qkv_weight, preferred_element_type=jnp.float32).reshape(
        rows, 3, heads, width
    )
    query = rms_gain(proj[:, 0], qk_gain[0])
    keyed = rms_gain(proj[:, 1], qk_gain[1])
    packed = (
        jnp.stack([query, keyed, proj[:, 2]], axis=1)
        .astype(jnp.bfloat16)
        .reshape(rows, 3, heads * width)
    )
    cond_rows = cond_kv.shape[0]
    cond = cond_kv.reshape(cond_rows, 2, heads, width)
    cond_key = rms_gain(cond[:, 0].astype(jnp.float32), qk_gain[1]).astype(jnp.bfloat16)
    cond_pack = jnp.stack([cond_key, cond[:, 1]], axis=1).reshape(cond_rows, 2, heads * width)
    sent, cond_sent = (
        lax.all_to_all(packed, "sub", split_axis=2, concat_axis=0, tiled=True),
        lax.all_to_all(cond_pack, "sub", split_axis=2, concat_axis=0, tiled=True),
    )
    operands, start_state, absorb = arrange(sent, cond_sent, width)
    carry = absorb(
        start_state,
        (
            lax.all_gather(operands[0], "seq", axis=0, tiled=True),
            lax.all_gather(operands[1], "seq", axis=0, tiled=True),
            lax.all_gather(operands[2], "seq", axis=0, tiled=True),
            lax.all_gather(operands[3], "seq", axis=0, tiled=True),
        ),
        jnp.int32(0),
    )
    attended = lax.all_to_all(finish(carry), "sub", split_axis=0, concat_axis=1, tiled=True)
    return jnp.dot(attended, out_weight, preferred_element_type=jnp.float32).astype(jnp.bfloat16)


LANES = 128


def pair_norm(field, gain, half):
    low = lax.broadcasted_iota(jnp.int32, field.shape, 1) < half
    squares = field * field
    first = jnp.sum(jnp.where(low, squares, 0.0), axis=-1, keepdims=True)
    second = jnp.sum(jnp.where(low, 0.0, squares), axis=-1, keepdims=True)
    mean = jnp.where(low, first, second) * (1.0 / half)
    return field * lax.rsqrt(mean + 1e-06) * gain


def joint_kernel(
    seq, sub, half,
    latent_hbm, cond_hbm, weight_hbm, gain_hbm, out_weight_hbm, out,
    latent, cond_kv, gain, weight, out_weight, send_kv, send_q, recv_kv, recv_q, value_t, answer, parts, attended,
    input_sem, weight_sem, out_weight_sem, kv_sent, kv_here, q_sent, q_here, answer_sent, part_here,
):
    across = sub // 2
    pairs = seq * across
    count = 2 * pairs
    width = count * half
    rows, cond_rows = latent.shape[0], cond_kv.shape[0]
    held = rows + cond_rows
    my_seq, my_sub = lax.axis_index("seq"), lax.axis_index("sub")
    my_side, my_up = my_sub // across, lax.rem(my_sub, across)
    mine = my_seq * across + my_up
    me = my_side * pairs + mine
    other = (1 - my_side) * pairs

    def device(slot):
        pair = lax.rem(slot, pairs)
        side = slot // pairs
        return {"seq": pair // across, "sub": side * across + lax.rem(pair, across)}

    def pair_to(step):
        up = lax.rem(my_up + 1 + step // seq, across)
        return lax.rem(my_seq + 1 + lax.rem(step, seq), seq) * across + up

    def pair_from(step):
        up = lax.rem(my_up + 2 * across - 1 - step // seq, across)
        return lax.rem(my_seq + seq - 1 - lax.rem(step, seq), seq) * across + up

    def load(step, part):
        column = pl.multiple_of(part * width + pair_to(step) * LANES, LANES)
        return pltpu.make_async_copy(
            weight_hbm.at[:, pl.ds(column, LANES)],
            weight.at[step, :, pl.ds(part * LANES, LANES)],
            weight_sem.at[step, part],
        )

    def start_load(step, unused):
        for part in range(3):
            load(step, part).start()
        return unused

    inputs = [
        pltpu.make_async_copy(source, target, input_sem.at[i])
        for i, (source, target) in enumerate(
            [(latent_hbm, latent), (cond_hbm, cond_kv), (gain_hbm, gain)]
        )
    ]
    for copy in inputs:
        copy.start()
    lax.fori_loop(0, 2, start_load, 0)
    out_load = pltpu.make_async_copy(out_weight_hbm, out_weight, out_weight_sem)

    barrier = pltpu.get_barrier_semaphore()

    def greet(slot, unused):
        @pl.when(slot != me)
        def _():
            pl.semaphore_signal(barrier, inc=1, device_id=device(slot))

        return unused

    lax.fori_loop(0, count, greet, 0)

    def kv_copy(pair, landing):
        return pltpu.make_async_remote_copy(
            src_ref=send_kv.at[pair], dst_ref=recv_kv.at[landing],
            send_sem=kv_sent.at[pair], recv_sem=kv_here.at[landing],
            device_id=device(my_side * pairs + pair),
        )

    def q_copy(slot, landing):
        return pltpu.make_async_remote_copy(
            src_ref=send_q.at[lax.rem(slot, pairs)], dst_ref=recv_q.at[landing],
            send_sem=q_sent.at[slot], recv_sem=q_here.at[landing],
            device_id=device(slot),
        )

    def answer_copy(slot, landing):
        return pltpu.make_async_remote_copy(
            src_ref=answer.at[slot], dst_ref=parts.at[landing],
            send_sem=answer_sent.at[slot], recv_sem=part_here.at[landing],
            device_id=device(slot),
        )

    scale = float(half) ** -0.5
    for copy in inputs:
        copy.wait()

    def project(step, unused):
        pair = pair_to(step)
        column = pl.multiple_of(pair * LANES, LANES)
        for part in range(3):
            load(step, part).wait()

        @pl.when(step + 2 < pairs)
        def _():
            for part in range(3):
                load(step + 2, part).start()

        @pl.when(step == pairs - 1)
        def _():
            out_load.start()

        proj = jnp.dot(latent[...], weight[step], preferred_element_type=jnp.float32)
        query_gain = jnp.concatenate([gain[0, pl.ds(2 * pair + i, 1)] for i in range(2)], axis=1)
        key_gain = jnp.concatenate([gain[1, pl.ds(2 * pair + i, 1)] for i in range(2)], axis=1)
        query = pair_norm(proj[:, :LANES], query_gain, half) * scale
        send_q[pair] = query.astype(jnp.bfloat16).T
        keyed = pair_norm(proj[:, LANES : 2 * LANES], key_gain, half)
        send_kv[pair, :rows] = keyed.astype(jnp.bfloat16)
        cond_field = cond_kv[:, :, pl.ds(column, LANES)].astype(jnp.float32)
        cond_keyed = pair_norm(cond_field[:, 0], key_gain, half)
        send_kv[pair, rows:held] = cond_keyed.astype(jnp.bfloat16)
        send_kv[pair, held : held + rows] = proj[:, 2 * LANES :].astype(jnp.bfloat16)
        send_kv[pair, held + rows :] = cond_field[:, 1].astype(jnp.bfloat16)

        @pl.when(step == 0)
        def _():
            pl.semaphore_wait(barrier, count - 1)

        @pl.when(pair != mine)
        def _():
            kv_copy(pair, mine).start()

        q_copy(other + pair, me).start()

        @pl.when(pair == mine)
        def _():
            recv_kv[mine] = send_kv[mine]
            recv_q[me] = send_q[mine]

        return unused

    lax.fori_loop(0, pairs, project, 0)

    def send_near(step, unused):
        q_copy(my_side * pairs + pair_to(step), me).start()
        return unused

    lax.fori_loop(0, pairs - 1, send_near, 0)

    def receive(pair, unused):
        @pl.when(pair != mine)
        def _():
            kv_copy(pair, pair).wait_recv()

        return unused

    lax.fori_loop(0, pairs, receive, 0)

    value_t[...] = recv_kv[:, held:, :].reshape(pairs * held, LANES).T

    def attend(slots):
        keyed = recv_kv[:, :held, :].reshape(pairs * held, LANES)
        values = value_t[...]
        scores = []
        for slot in slots:
            query = recv_q[slot]
            low = lax.broadcasted_iota(jnp.int32, query.shape, 0) < half
            empty = jnp.zeros_like(query)
            query = jnp.concatenate(
                [jnp.where(low, query, empty), jnp.where(low, empty, query)], axis=1
            )
            scores.append(jnp.dot(keyed, query, preferred_element_type=jnp.float32))
        results = []
        for score in scores:
            highest = jnp.max(score, axis=0, keepdims=True)
            expd = jnp.exp(score - highest)
            total = jnp.sum(expd, axis=0, keepdims=True)
            summed = jnp.dot(
                values, expd.astype(jnp.bfloat16), preferred_element_type=jnp.float32
            )
            results.append((summed, highest, total))
        for slot, (summed, highest, total) in zip(slots, results):
            result = summed / total
            answer[slot, :half] = result[:half, :rows].astype(jnp.bfloat16)
            answer[slot, half : 2 * half] = result[half:, rows:].astype(jnp.bfloat16)
            left = highest + jnp.log(total)
            terms = []
            for unused in range(3):
                term = left.astype(jnp.bfloat16).astype(jnp.float32)
                left = left - term
                terms += [term[:, :rows], term[:, rows:]]
            terms.append(jnp.zeros((8 - len(terms), rows), jnp.float32))
            answer[slot, 2 * half :] = jnp.concatenate(terms, axis=0).astype(jnp.bfloat16)

    def attend_far(step, unused):
        slots = [other + pair_from(2 * step + i) for i in range(2)]
        for slot in slots:
            q_copy(slot, slot).wait_recv()
        attend(slots)
        for slot in slots:
            answer_copy(slot, me).start()
        return unused

    lax.fori_loop(0, pairs // 2, attend_far, 0)

    def attend_near(step, unused):
        slots = [my_side * pairs + pair_from(2 * step + i) for i in range(2)]
        for slot in slots:

            @pl.when(slot != me)
            def _():
                q_copy(slot, slot).wait_recv()

        attend(slots)
        for slot in slots:

            @pl.when(slot != me)
            def _():
                answer_copy(slot, me).start()

            @pl.when(slot == me)
            def _():
                parts[me] = answer[me]

        return unused

    lax.fori_loop(0, pairs // 2, attend_near, 0)
    out_load.wait()

    def logs(slot):
        stats = parts[slot, 2 * half :].astype(jnp.float32)
        return stats[0:2] + stats[2:4] + stats[4:6]

    def merge(step, unused):
        pair = pair_to(step)
        near, far = my_side * pairs + pair, other + pair
        answer_copy(far, far).wait_recv()

        @pl.when(near != me)
        def _():
            answer_copy(near, near).wait_recv()

        first, second = logs(near), logs(far)
        highest = jnp.maximum(first, second)
        first, second = jnp.exp(first - highest), jnp.exp(second - highest)
        both = first + second
        first, second = first / both, second / both
        merged = []
        for head in range(2):
            span = slice(head * half, (head + 1) * half)
            merged.append(
                parts[near, span].astype(jnp.float32) * first[head : head + 1]
                + parts[far, span].astype(jnp.float32) * second[head : head + 1]
            )
        merged = jnp.concatenate(merged, axis=0).astype(jnp.bfloat16)
        column = pl.multiple_of(pair * LANES, LANES)
        attended[:, pl.ds(column, LANES)] = merged.T
        return unused

    lax.fori_loop(0, pairs, merge, 0)

    out[...] = jnp.dot(
        attended[...], out_weight[...], preferred_element_type=jnp.float32
    ).astype(jnp.bfloat16)

    def drain(slot, unused):
        q_pair = lax.rem(slot, pairs)

        @pl.when(slot != me)
        def _():
            q_copy(slot, slot).wait_send()
            answer_copy(slot, slot).wait_send()

        @pl.when(jnp.logical_and(slot < pairs, q_pair != mine))
        def _():
            kv_copy(q_pair, q_pair).wait_send()

        return unused

    lax.fori_loop(0, count, drain, 0)


def pair_each(seq, sub, latent, cond_kv, qkv_weight, qk_gain, out_weight):
    rows, depth = latent.shape
    heads, half = qk_gain.shape[1:]
    cond_rows = cond_kv.shape[0]
    count = seq * sub
    pairs = count // 2
    held = rows + cond_rows
    vmem = pl.BlockSpec(memory_space=pltpu.VMEM)
    hbm = pl.BlockSpec(memory_space=pltpu.HBM)
    narrow = jnp.bfloat16
    return pl.pallas_call(
        functools.partial(joint_kernel, seq, sub, half),
        out_shape=jax.ShapeDtypeStruct((rows, out_weight.shape[1]), narrow),
        in_specs=[hbm] * 5,
        out_specs=vmem,
        scratch_shapes=[
            pltpu.VMEM(latent.shape, narrow),
            pltpu.VMEM(cond_kv.shape, narrow),
            pltpu.VMEM(qk_gain.shape, jnp.float32),
            pltpu.VMEM((pairs, depth, 3 * LANES), narrow),
            pltpu.VMEM(out_weight.shape, narrow),
            pltpu.VMEM((pairs, 2 * held, LANES), narrow),
            pltpu.VMEM((pairs, LANES, rows), narrow),
            pltpu.VMEM((pairs, 2 * held, LANES), narrow),
            pltpu.VMEM((count, LANES, rows), narrow),
            pltpu.VMEM((LANES, pairs * held), narrow),
            pltpu.VMEM((count, LANES + 8, rows), narrow),
            pltpu.VMEM((count, LANES + 8, rows), narrow),
            pltpu.VMEM((rows, heads * half), narrow),
            pltpu.SemaphoreType.DMA((3,)),
            pltpu.SemaphoreType.DMA((pairs, 3)),
            pltpu.SemaphoreType.DMA,
            pltpu.SemaphoreType.DMA((pairs,)),
            pltpu.SemaphoreType.DMA((pairs,)),
            pltpu.SemaphoreType.DMA((count,)),
            pltpu.SemaphoreType.DMA((count,)),
            pltpu.SemaphoreType.DMA((count,)),
            pltpu.SemaphoreType.DMA((count,)),
        ],
        compiler_params=pltpu.CompilerParams(
            collective_id=0, has_side_effects=True, vmem_limit_bytes=44 * 1024 * 1024
        ),
    )(
        *(
            pltpu.with_memory_space_constraint(array, pltpu.HBM)
            for array in (latent, cond_kv, qkv_weight, qk_gain, out_weight)
        )
    )


def layer(seq, sub, latent, cond_kv, qkv_weight, qk_gain, out_weight):
    heads, width = qk_gain.shape[1:]
    fits = heads == seq * sub and 2 * width == LANES and latent.shape[0] == LANES
    fits = fits and sub % 2 == 0 and seq % 2 == 0 and cond_kv.shape[0] % 16 == 0
    if fits:
        return pair_each(seq, sub, latent, cond_kv, qkv_weight, qk_gain, out_weight)
    return local(latent, cond_kv, qkv_weight, qk_gain, out_weight)


def solution(mesh):
    return jax.shard_map(
        functools.partial(layer, mesh.shape["seq"], mesh.shape["sub"]),
        mesh=mesh,
        in_specs=(
            P(("clip", "seq", "sub"), None),
            P(("clip", "seq", "sub"), None, None),
            P(),
            P(),
            P(),
        ),
        out_specs=P(("clip", "seq", "sub"), None),
        check_vma=False,
    )
```

```python
import functools

import jax
import jax.numpy as jnp
from jax import lax
from jax.experimental import pallas as pl
from jax.experimental.pallas import tpu as pltpu
from jax.sharding import PartitionSpec as P


def rms_gain(field, gain):
    return field * lax.rsqrt(jnp.mean(field * field, axis=-1, keepdims=True) + 1e-06) * gain


def update(carry, query, key_block, value_block):
    highest, total, summed = carry
    scale = 1.0 / jnp.sqrt(jnp.float32(query.shape[-1]))
    scores = (
        jnp.einsum("qhd,khd->hqk", query, key_block, preferred_element_type=jnp.float32) * scale
    )
    new_high = jnp.maximum(highest, jnp.max(scores, axis=-1))
    expd = jnp.exp(scores - new_high[..., None])
    factor = jnp.exp(highest - new_high)
    total = total * factor + jnp.sum(expd, axis=-1)
    summed = summed * factor[..., None] + jnp.einsum(
        "hqk,khd->hqd", expd.astype(jnp.bfloat16), value_block, preferred_element_type=jnp.float32
    )
    return (new_high, total, summed)


def fold_rows(carry, query, keys_piece, values_piece, block_rows):
    count = keys_piece.shape[0] // block_rows
    key_blocks = keys_piece.reshape((count, block_rows) + keys_piece.shape[1:])
    value_blocks = values_piece.reshape((count, block_rows) + values_piece.shape[1:])

    def advance(state, pair):
        return (update(state, query, pair[0], pair[1]), None)

    carry, unused = lax.scan(advance, carry, (key_blocks, value_blocks))
    return carry


def arrange(sent, cond_sent, width):
    queries = sent.shape[0]
    local_heads = sent.shape[2] // width
    query = sent[:, 0].reshape(queries, local_heads, width)
    keyed = sent[:, 1].reshape(queries, local_heads, width)
    valued = sent[:, 2].reshape(queries, local_heads, width)
    cond_rows = cond_sent.shape[0]
    cond_key = cond_sent[:, 0].reshape(cond_rows, local_heads, width)
    cond_value = cond_sent[:, 1].reshape(cond_rows, local_heads, width)
    start_state = (
        jnp.full((local_heads, queries), -1e30, jnp.float32),
        jnp.zeros((local_heads, queries), jnp.float32),
        jnp.zeros((local_heads, queries, width), jnp.float32),
    )

    def absorb(carry, pieces, start):
        carry = fold_rows(carry, query, pieces[0], pieces[1], queries)
        return fold_rows(carry, query, pieces[2], pieces[3], cond_rows)

    return ((keyed, valued, cond_key, cond_value), start_state, absorb)


def finish(carry):
    highest, total, summed = carry
    attended = summed / total[..., None]
    local_heads, queries, width = attended.shape
    return attended.transpose(1, 0, 2).reshape(queries, local_heads * width).astype(jnp.bfloat16)


def local(latent, cond_kv, qkv_weight, qk_gain, out_weight):
    rows = latent.shape[0]
    heads = qk_gain.shape[1]
    width = qk_gain.shape[2]
    proj = jnp.dot(latent, qkv_weight, preferred_element_type=jnp.float32).reshape(
        rows, 3, heads, width
    )
    query = rms_gain(proj[:, 0], qk_gain[0])
    keyed = rms_gain(proj[:, 1], qk_gain[1])
    packed = (
        jnp.stack([query, keyed, proj[:, 2]], axis=1)
        .astype(jnp.bfloat16)
        .reshape(rows, 3, heads * width)
    )
    cond_rows = cond_kv.shape[0]
    cond = cond_kv.reshape(cond_rows, 2, heads, width)
    cond_key = rms_gain(cond[:, 0].astype(jnp.float32), qk_gain[1]).astype(jnp.bfloat16)
    cond_pack = jnp.stack([cond_key, cond[:, 1]], axis=1).reshape(cond_rows, 2, heads * width)
    sent, cond_sent = (
        lax.all_to_all(packed, "sub", split_axis=2, concat_axis=0, tiled=True),
        lax.all_to_all(cond_pack, "sub", split_axis=2, concat_axis=0, tiled=True),
    )
    operands, start_state, absorb = arrange(sent, cond_sent, width)
    carry = absorb(
        start_state,
        (
            lax.all_gather(operands[0], "seq", axis=0, tiled=True),
            lax.all_gather(operands[1], "seq", axis=0, tiled=True),
            lax.all_gather(operands[2], "seq", axis=0, tiled=True),
            lax.all_gather(operands[3], "seq", axis=0, tiled=True),
        ),
        jnp.int32(0),
    )
    attended = lax.all_to_all(finish(carry), "sub", split_axis=0, concat_axis=1, tiled=True)
    return jnp.dot(attended, out_weight, preferred_element_type=jnp.float32).astype(jnp.bfloat16)


LANES = 128


def pair_norm(field, gain, half):
    low = lax.broadcasted_iota(jnp.int32, field.shape, 1) < half
    squares = field * field
    first = jnp.sum(jnp.where(low, squares, 0.0), axis=-1, keepdims=True)
    second = jnp.sum(jnp.where(low, 0.0, squares), axis=-1, keepdims=True)
    mean = jnp.where(low, first, second) * (1.0 / half)
    return field * lax.rsqrt(mean + 1e-06) * gain


def joint_kernel(
    seq, sub, half,
    latent_hbm, cond_hbm, weight_hbm, gain_hbm, out_weight_hbm, out,
    latent, cond_kv, gain, weight, out_weight, send_kv_ref, send_q, recv_kv, recv_q, value_t, answer, parts, relayed, attended,
    input_sem, weight_sem, out_weight_sem, kv_sent, kv_here, q_sent, q_here, answer_sent, part_here, relay_here, ready,
):
    across = sub // 2
    pairs = seq * across
    count = 2 * pairs
    width = count * half
    rows, cond_rows = latent.shape[0], cond_kv.shape[0]
    held = rows + cond_rows
    my_seq, my_sub = lax.axis_index("seq"), lax.axis_index("sub")
    my_side, my_up = my_sub // across, lax.rem(my_sub, across)
    mine = my_seq * across + my_up
    me = my_side * pairs + mine
    other = (1 - my_side) * pairs

    def device(slot):
        pair = lax.rem(slot, pairs)
        side = slot // pairs
        return {"seq": pair // across, "sub": side * across + lax.rem(pair, across)}

    def pair_to(step):
        up = lax.rem(my_up + 1 + step // seq, across)
        return lax.rem(my_seq + 1 + lax.rem(step, seq), seq) * across + up

    def load(step, part):
        column = pl.multiple_of(part * width + pair_to(step) * LANES, LANES)
        return pltpu.make_async_copy(
            weight_hbm.at[:, pl.ds(column, LANES)],
            weight.at[step, :, pl.ds(part * LANES, LANES)],
            weight_sem.at[step, part],
        )

    def start_load(step, unused):
        for part in range(3):
            load(step, part).start()
        return unused

    inputs = [
        pltpu.make_async_copy(source, target, input_sem.at[i])
        for i, (source, target) in enumerate(
            [(latent_hbm, latent), (cond_hbm, cond_kv), (gain_hbm, gain)]
        )
    ]
    for copy in inputs:
        copy.start()
    lax.fori_loop(0, 2, start_load, 0)
    out_load = pltpu.make_async_copy(out_weight_hbm, out_weight, out_weight_sem)

    barrier = pltpu.get_barrier_semaphore()

    def greet(slot, unused):
        later = jnp.logical_or(my_side == 0, slot // pairs == 1)

        @pl.when(jnp.logical_and(slot != me, later))
        def _():
            pl.semaphore_signal(barrier, inc=1, device_id=device(slot))

        return unused

    def announce(slot, unused):
        pl.semaphore_signal(ready, inc=1, device_id=device(slot))
        return unused

    lax.fori_loop(0, count, greet, 0)

    def kv_copy(pair, landing):
        return pltpu.make_async_remote_copy(
            src_ref=send_kv_ref.at[pair], dst_ref=recv_kv.at[landing],
            send_sem=kv_sent.at[pair], recv_sem=kv_here.at[landing],
            device_id=device(my_side * pairs + pair),
        )

    def q_copy(slot, landing):
        return pltpu.make_async_remote_copy(
            src_ref=send_q.at[lax.rem(slot, pairs)], dst_ref=recv_q.at[landing],
            send_sem=q_sent.at[slot], recv_sem=q_here.at[landing],
            device_id=device(slot),
        )

    def answer_copy(slot, landing):
        return pltpu.make_async_remote_copy(
            src_ref=answer.at[slot], dst_ref=parts.at[landing],
            send_sem=answer_sent.at[slot], recv_sem=part_here.at[landing],
            device_id=device(slot),
        )

    outer = my_up == my_side

    def relay_copy(slot):
        seat = lax.rem(slot, pairs) // across
        return pltpu.make_async_remote_copy(
            src_ref=answer.at[slot], dst_ref=relayed.at[seat],
            send_sem=answer_sent.at[slot], recv_sem=relay_here.at[seat],
            device_id={"seq": my_seq, "sub": (1 - my_side) * across + my_side},
        )

    scale = float(half) ** -0.5
    for copy in inputs:
        copy.wait()

    def project(step, unused):
        pair = pair_to(step)
        column = pl.multiple_of(pair * LANES, LANES)
        for part in range(3):
            load(step, part).wait()

        @pl.when(step + 2 < pairs)
        def _():
            for part in range(3):
                load(step + 2, part).start()

        @pl.when(step == pairs - 1)
        def _():
            out_load.start()

        proj = jnp.dot(latent[...], weight[step], preferred_element_type=jnp.float32)
        query_gain = jnp.concatenate([gain[0, pl.ds(2 * pair + i, 1)] for i in range(2)], axis=1)
        key_gain = jnp.concatenate([gain[1, pl.ds(2 * pair + i, 1)] for i in range(2)], axis=1)
        query = pair_norm(proj[:, :LANES], query_gain, half) * scale
        send_q[pair] = query.astype(jnp.bfloat16).T
        keyed = pair_norm(proj[:, LANES : 2 * LANES], key_gain, half)
        send_kv_ref[pair, :rows] = keyed.astype(jnp.bfloat16)
        cond_field = cond_kv[:, :, pl.ds(column, LANES)].astype(jnp.float32)
        cond_keyed = pair_norm(cond_field[:, 0], key_gain, half)
        send_kv_ref[pair, rows:held] = cond_keyed.astype(jnp.bfloat16)
        send_kv_ref[pair, held : held + rows] = proj[:, 2 * LANES :].astype(jnp.bfloat16)
        send_kv_ref[pair, held + rows :] = cond_field[:, 1].astype(jnp.bfloat16)

        @pl.when(step == start)
        def _():
            @pl.when(my_side == 0)
            def _():
                pl.semaphore_wait(barrier, pairs - 1)

            @pl.when(my_side == 1)
            def _():
                pl.semaphore_wait(barrier, count - 1)
                lax.fori_loop(0, pairs, announce, 0)

            lax.fori_loop(0, step, send_kv, 0)

        @pl.when(step >= start)
        def _():
            send_kv(step, 0)

        @pl.when(step == opening)
        def _():
            @pl.when(my_side == 0)
            def _():
                pl.semaphore_wait(ready, pairs)

            lax.fori_loop(0, step, send_far, 0)

        @pl.when(step >= opening)
        def _():
            send_far(step, 0)

        return unused

    def send_kv(step, unused):
        pair = pair_to(step)

        @pl.when(pair != mine)
        def _():
            kv_copy(pair, mine).start()

        @pl.when(pair == mine)
        def _():
            recv_kv[mine] = send_kv_ref[mine]
            recv_q[me] = send_q[mine]

        return unused

    def send_far(step, unused):
        q_copy(other + pair_to(step), me).start()
        return unused

    start = jnp.where(my_sub == 0, 2, jnp.where(my_sub == 1, 0, 0))
    late_opening = jnp.where(my_sub == across, 0, 7)
    early_opening = jnp.where(my_sub == 0, 6, 5)
    opening = jnp.where(my_side == 0, early_opening, late_opening)
    lax.fori_loop(0, pairs, project, 0)

    def send_near(step, unused):
        q_copy(my_side * pairs + pair_to(step), me).start()
        return unused

    lax.fori_loop(0, pairs - 1, send_near, 0)

    def receive(pair, unused):
        @pl.when(pair != mine)
        def _():
            kv_copy(pair, pair).wait_recv()

        return unused

    lax.fori_loop(0, pairs, receive, 0)

    value_t[...] = recv_kv[:, held:, :].reshape(pairs * held, LANES).T

    def attend(slots):
        keyed = recv_kv[:, :held, :].reshape(pairs * held, LANES)
        values = value_t[...]
        scores = []
        for slot in slots:
            query = recv_q[slot]
            low = lax.broadcasted_iota(jnp.int32, query.shape, 0) < half
            empty = jnp.zeros_like(query)
            query = jnp.concatenate(
                [jnp.where(low, query, empty), jnp.where(low, empty, query)], axis=1
            )
            scores.append(jnp.dot(keyed, query, preferred_element_type=jnp.float32))
        results = []
        for score in scores:
            highest = jnp.max(score, axis=0, keepdims=True)
            expd = jnp.exp(score - highest)
            total = jnp.sum(expd, axis=0, keepdims=True)
            summed = jnp.dot(
                values, expd.astype(jnp.bfloat16), preferred_element_type=jnp.float32
            )
            results.append((summed, highest, total))
        for slot, (summed, highest, total) in zip(slots, results):
            result = summed / total
            answer[slot, :half] = result[:half, :rows].astype(jnp.bfloat16)
            answer[slot, half : 2 * half] = result[half:, rows:].astype(jnp.bfloat16)
            left = highest + jnp.log(total)
            terms = []
            for unused in range(3):
                term = left.astype(jnp.bfloat16).astype(jnp.float32)
                left = left - term
                terms += [term[:, :rows], term[:, rows:]]
            terms.append(jnp.zeros((8 - len(terms), rows), jnp.float32))
            answer[slot, 2 * half :] = jnp.concatenate(terms, axis=0).astype(jnp.bfloat16)

    def pick(table, quarter):
        chosen = 0
        for place in range(sub):
            for i in range(4):
                here = jnp.logical_and(my_sub == place, quarter == i)
                chosen = jnp.where(here, table[place][i], chosen)
        return chosen

    def slot_at(turn, i):
        place = 2 * turn + i
        quarter = place // seq
        far = pick([(1, 1, 0, 0), (1, 1, 0, 0), (1, 1, 0, 0), (1, 0, 1, 0)], quarter)
        up = lax.rem(my_up + pick([(1, 0, 0, 1), (1, 0, 1, 0), (1, 0, 1, 0), (1, 1, 0, 0)], quarter), across)
        seat = lax.rem(my_seq + 2 * seq - 1 - lax.rem(place, seq), seq)
        return lax.rem(my_side + far, 2) * pairs + seat * across + up

    def logs(stats):
        stats = stats.astype(jnp.float32)
        return stats[0:2] + stats[2:4] + stats[4:6]

    def combine(near, far):
        first, second = logs(near[2 * half :]), logs(far[2 * half :])
        highest = jnp.maximum(first, second)
        first, second = jnp.exp(first - highest), jnp.exp(second - highest)
        both = first + second
        first, second = first / both, second / both
        merged = []
        for head in range(2):
            span = slice(head * half, (head + 1) * half)
            merged.append(
                near[span].astype(jnp.float32) * first[head : head + 1]
                + far[span].astype(jnp.float32) * second[head : head + 1]
            )
        return jnp.concatenate(merged, axis=0).astype(jnp.bfloat16)

    def take(turn, unused):
        slots = [slot_at(turn, i) for i in range(2)]
        for slot in slots:

            @pl.when(slot != me)
            def _():
                q_copy(slot, slot).wait_recv()

        attend(slots)
        for slot in slots:
            side, up = slot // pairs, lax.rem(slot, across)
            passing = jnp.logical_and(outer, side != my_side)
            passing = jnp.logical_and(passing, up != my_side)
            joining = jnp.logical_and(my_up != my_side, side == my_side)
            joining = jnp.logical_and(joining, up == my_side)

            @pl.when(joining)
            def _():
                relay_copy(slot).wait_recv()
                seat = lax.rem(slot, pairs) // across
                answer[slot, : 2 * half] = combine(answer[slot], relayed[seat])

            @pl.when(passing)
            def _():
                relay_copy(slot).start()

            @pl.when(jnp.logical_and(slot != me, jnp.logical_not(passing)))
            def _():
                answer_copy(slot, me).start()

            @pl.when(slot == me)
            def _():
                parts[me] = answer[me]

        return unused

    lax.fori_loop(0, pairs, take, 0)
    out_load.wait()

    def merge(step, unused):
        pair = pair_to(step)
        near, far = my_side * pairs + pair, other + pair
        column = pl.multiple_of(pair * LANES, LANES)
        whole = jnp.logical_and(outer, lax.rem(pair, across) != my_up)

        @pl.when(near != me)
        def _():
            answer_copy(near, near).wait_recv()

        @pl.when(whole)
        def _():
            attended[:, pl.ds(column, LANES)] = parts[near, : 2 * half].T

        @pl.when(jnp.logical_not(whole))
        def _():
            answer_copy(far, far).wait_recv()
            attended[:, pl.ds(column, LANES)] = combine(parts[near], parts[far]).T

        return unused

    lax.fori_loop(0, pairs, merge, 0)

    out[...] = jnp.dot(
        attended[...], out_weight[...], preferred_element_type=jnp.float32
    ).astype(jnp.bfloat16)

    def drain(slot, unused):
        q_pair = lax.rem(slot, pairs)

        @pl.when(slot != me)
        def _():
            q_copy(slot, slot).wait_send()
            answer_copy(slot, slot).wait_send()

        @pl.when(jnp.logical_and(slot < pairs, q_pair != mine))
        def _():
            kv_copy(q_pair, q_pair).wait_send()

        return unused

    lax.fori_loop(0, count, drain, 0)


def pair_each(seq, sub, latent, cond_kv, qkv_weight, qk_gain, out_weight):
    rows, depth = latent.shape
    heads, half = qk_gain.shape[1:]
    cond_rows = cond_kv.shape[0]
    count = seq * sub
    pairs = count // 2
    held = rows + cond_rows
    vmem = pl.BlockSpec(memory_space=pltpu.VMEM)
    hbm = pl.BlockSpec(memory_space=pltpu.HBM)
    narrow = jnp.bfloat16
    return pl.pallas_call(
        functools.partial(joint_kernel, seq, sub, half),
        out_shape=jax.ShapeDtypeStruct((rows, out_weight.shape[1]), narrow),
        in_specs=[hbm] * 5,
        out_specs=vmem,
        scratch_shapes=[
            pltpu.VMEM(latent.shape, narrow),
            pltpu.VMEM(cond_kv.shape, narrow),
            pltpu.VMEM(qk_gain.shape, jnp.float32),
            pltpu.VMEM((pairs, depth, 3 * LANES), narrow),
            pltpu.VMEM(out_weight.shape, narrow),
            pltpu.VMEM((pairs, 2 * held, LANES), narrow),
            pltpu.VMEM((pairs, LANES, rows), narrow),
            pltpu.VMEM((pairs, 2 * held, LANES), narrow),
            pltpu.VMEM((count, LANES, rows), narrow),
            pltpu.VMEM((LANES, pairs * held), narrow),
            pltpu.VMEM((count, LANES + 8, rows), narrow),
            pltpu.VMEM((count, LANES + 8, rows), narrow),
            pltpu.VMEM((seq, LANES + 8, rows), narrow),
            pltpu.VMEM((rows, heads * half), narrow),
            pltpu.SemaphoreType.DMA((3,)),
            pltpu.SemaphoreType.DMA((pairs, 3)),
            pltpu.SemaphoreType.DMA,
            pltpu.SemaphoreType.DMA((pairs,)),
            pltpu.SemaphoreType.DMA((pairs,)),
            pltpu.SemaphoreType.DMA((count,)),
            pltpu.SemaphoreType.DMA((count,)),
            pltpu.SemaphoreType.DMA((count,)),
            pltpu.SemaphoreType.DMA((count,)),
            pltpu.SemaphoreType.DMA((seq,)),
            pltpu.SemaphoreType.REGULAR,
        ],
        compiler_params=pltpu.CompilerParams(
            collective_id=0, has_side_effects=True, vmem_limit_bytes=44 * 1024 * 1024
        ),
    )(
        *(
            pltpu.with_memory_space_constraint(array, pltpu.HBM)
            for array in (latent, cond_kv, qkv_weight, qk_gain, out_weight)
        )
    )


def layer(seq, sub, latent, cond_kv, qkv_weight, qk_gain, out_weight):
    heads, width = qk_gain.shape[1:]
    fits = heads == seq * sub and 2 * width == LANES and latent.shape[0] == LANES
    fits = fits and sub == 4 and seq % 2 == 0 and cond_kv.shape[0] % 16 == 0
    if fits:
        return pair_each(seq, sub, latent, cond_kv, qkv_weight, qk_gain, out_weight)
    return local(latent, cond_kv, qkv_weight, qk_gain, out_weight)


def solution(mesh):
    return jax.shard_map(
        functools.partial(layer, mesh.shape["seq"], mesh.shape["sub"]),
        mesh=mesh,
        in_specs=(
            P(("clip", "seq", "sub"), None),
            P(("clip", "seq", "sub"), None, None),
            P(),
            P(),
            P(),
        ),
        out_specs=P(("clip", "seq", "sub"), None),
        check_vma=False,
    )
```
